32 devices in a mesh: row: 4 (over y, x), col: 8 (over z, core).
Axes of the slice: x: 2, y: 2, z: 4, core: 2. Of those that a mesh axis runs over, the one named last changes fastest.
Arguments:
- incoming_optic_cosine_part: float32 [2048, 2048], P('row', 'col'), may hold values from -6 to 6
- incoming_optic_sine_part: float32 [2048, 2048], P('row', 'col'), may hold values from -6 to 6
- weak_pulse_growth_rate: float32 [2048, 2048], P('row', 'col'), may hold values from 0.5 to 2
- thermal_rise_beforehand: float32 [8, 2048, 2048], P('row', None, 'col'), may hold values from -6 to 6
- lengthwise_slice_pick: int32 [2], replicated, may hold values from 0 to 7
Outputs:
- temperature_out: float32 [8, 2048, 2048], P('row', None, 'col')
- beam_out_real: float32 [2048, 2048], P('row', 'col')
- beam_out_imag: float32 [2048, 2048], P('row', 'col')
The draws below stay inside these ranges and needn't reach their ends.
Inputs may be any that keep to these rules, and one draw needn't show every extreme that they name: Step k deposits into plane lengthwise_slice_pick[k]; planes may repeat.
All inputs are finite; a program needn't handle non-finite values.
Results may differ from the reference program's by a relative error of at most 0.0001.
Values sent between devices are 32-bit elements; how exact they have to be, the bound alone decides.
A program may use at most 192 MiB of HBM per device.

```python
import math
import jax
import jax.numpy as jnp
from jax import lax

MESH_WIDTH = 2048
STEPS = 2
SWEEPS = 2
AXIAL_LAYER_NUM = 8


def levels(key, extent, cuts, least, high):
    def one(position, parts):
        heights = jax.random.uniform(jax.random.fold_in(jax.random.fold_in(key, 6), position), (parts,), jnp.float32, least / len(cuts), high / len(cuts))
        return jnp.repeat(jnp.exp(heights), extent[position] // parts).reshape((-1,) + (1,) * (len(extent) - position - 1))

    loudness = one(*cuts[0])
    for cut in cuts[1:]:
        loudness = loudness * one(*cut)
    return loudness


def normal_values(own_key, extent, width, bound, split=(), kind=jnp.bfloat16):
    array = width * jax.random.normal(own_key, extent, jnp.float32)
    if split:
        array = array * levels(own_key, extent, split, -0.22, 0.18)
    return jnp.clip(array, -bound, bound).astype(kind)


def setup_inputs(seed: int = 0) -> dict:
    key_list = jax.random.split(jax.random.key(seed), 6)
    incoming_optic_cosine_part = normal_values(key_list[0], (MESH_WIDTH, MESH_WIDTH), 1.0, 6.0, ((0, 4), (1, 8)), jnp.float32)
    incoming_optic_sine_part = normal_values(key_list[1], (MESH_WIDTH, MESH_WIDTH), 1.0, 6.0, ((0, 4), (1, 8)), jnp.float32)
    weak_pulse_growth_rate = jnp.clip(jnp.exp(math.log(2.0) - 1.3862944 * jax.random.uniform(key_list[2], (MESH_WIDTH, MESH_WIDTH), jnp.float32) ** levels(key_list[2], (MESH_WIDTH, MESH_WIDTH), ((0, 4), (1, 8)), -0.2, 0.2)), 0.5, 2.0)
    thermal_rise_beforehand = normal_values(key_list[3], (AXIAL_LAYER_NUM, MESH_WIDTH, MESH_WIDTH), 1.0, 6.0, ((0, 4), (2, 8)), jnp.float32)
    lengthwise_slice_pick = jax.random.randint(key_list[4], (STEPS,), 0, AXIAL_LAYER_NUM).astype(jnp.int32)
    return {"incoming_optic_cosine_part": incoming_optic_cosine_part, "incoming_optic_sine_part": incoming_optic_sine_part, "weak_pulse_growth_rate": weak_pulse_growth_rate, "thermal_rise_beforehand": thermal_rise_beforehand, "lengthwise_slice_pick": lengthwise_slice_pick}


FLUENCE_LIMIT = 2.0
GAIN_LENGTH = 0.2
INDEX_SLOPE_DNDT = 0.3


def adjacent_cells(border_extended):
    total = border_extended[2:, 1:-1, 1:-1] + border_extended[:-2, 1:-1, 1:-1]
    total = total + border_extended[1:-1, 2:, 1:-1] + border_extended[1:-1, :-2, 1:-1]
    total = total + border_extended[1:-1, 1:-1, 2:] + border_extended[1:-1, 1:-1, :-2]
    return total


def reference(incoming_optic_cosine_part, incoming_optic_sine_part, weak_pulse_growth_rate, thermal_rise_beforehand, lengthwise_slice_pick):
    field = lax.complex(incoming_optic_cosine_part, incoming_optic_sine_part)
    freq = jnp.arange(MESH_WIDTH, dtype=jnp.int32)
    modulus = 2 * MESH_WIDTH
    squares = (freq * freq) % modulus
    phase_index = (squares[:, None] + squares[None, :]) % modulus
    phase = math.pi * phase_index.astype(jnp.float32) / MESH_WIDTH
    kernel = lax.complex(jnp.cos(phase), -jnp.sin(phase))
    heats = []
    for step in range(STEPS):
        field = jnp.fft.ifft2(jnp.fft.fft2(field) * kernel)
        irradiance = jnp.real(field) ** 2 + jnp.imag(field) ** 2
        bleaching_factor = weak_pulse_growth_rate / (1.0 + irradiance / FLUENCE_LIMIT)
        heats.append(bleaching_factor * irradiance)
        field = field * jnp.exp(0.5 * GAIN_LENGTH * bleaching_factor)
    planes = jnp.arange(AXIAL_LAYER_NUM, dtype=jnp.int32)
    deposited_power = jnp.zeros(thermal_rise_beforehand.shape, jnp.float32)
    for step in range(STEPS):
        select = (planes == lengthwise_slice_pick[step]).astype(jnp.float32)
        deposited_power = deposited_power + select[:, None, None] * heats[step][None]
    linear_system_target = thermal_rise_beforehand + deposited_power
    present_warmth = thermal_rise_beforehand
    for sweep in range(SWEEPS):
        present_warmth = (linear_system_target + adjacent_cells(jnp.pad(present_warmth, 1))) / 7.0
    phase_angle = INDEX_SLOPE_DNDT * jnp.sum(present_warmth, axis=0)
    leaving_inphase = jnp.real(field) * jnp.cos(phase_angle) - jnp.imag(field) * jnp.sin(phase_angle)
    leaving_quadrature = jnp.real(field) * jnp.sin(phase_angle) + jnp.imag(field) * jnp.cos(phase_angle)
    return present_warmth, leaving_inphase, leaving_quadrature
```

```python
import functools
import math

import jax
import jax.numpy as jnp
from jax import lax
from jax.experimental import pallas as pl
from jax.experimental.pallas import tpu as pltpu
from jax.sharding import PartitionSpec as P

STEPS = 2
FLUENCE_LIMIT = 2.0
GAIN_LENGTH = 0.2
INDEX_SLOPE_DNDT = 0.3
RADIX = 8
VMEM = pl.BlockSpec(memory_space=pltpu.VMEM)


def swap(z):
    half = z.shape[-1] // 2
    if z.shape[-1] % 128 == 0:
        return pltpu.roll(z, half, z.ndim - 1)
    return jnp.concatenate([z[:, half:], z[:, :half]], axis=1)


def cmul(z, cosine, signed_sine):
    return z * cosine + swap(z) * signed_sine


def sign_row(width, first):
    lane = lax.broadcasted_iota(jnp.int32, (1, width), 1)
    return jnp.where(lane < width // 2, first, -first).astype(jnp.float32)


def dft8(z):
    width = z[0].shape[-1]
    sgn = sign_row(width, 1.0)
    root = math.sqrt(0.5)

    def rot(v):
        return swap(v) * sgn

    def dft4(p, q, r, s):
        a, b = p + r, p - r
        c, d = q + s, rot(q - s)
        return a + c, b + d, a - c, b - d

    even = dft4(z[0], z[2], z[4], z[6])
    odd = dft4(z[1], z[3], z[5], z[7])
    turned = (
        odd[0],
        (odd[1] + rot(odd[1])) * root,
        rot(odd[2]),
        (rot(odd[3]) - odd[3]) * root,
    )
    return [even[i] + turned[i] for i in range(4)] + [even[i] - turned[i] for i in range(4)]


def split2(x):
    high = x.astype(jnp.bfloat16)
    low = (x - high.astype(jnp.float32)).astype(jnp.bfloat16)
    return high, low


def fresnel_body(gain, *refs):
    if gain:
        x, prec, pres, whi, wlo, twc, tws, postc, posts, g, out, heat, mid = refs
    else:
        x, prec, pres, whi, wlo, twc, tws, postc, posts, out, mid = refs
    size = x.shape[1]
    width = x.shape[2]
    neg = sign_row(width, -1.0)

    def column(n1, carry):
        v = cmul(x[n1], prec[n1], pres[n1])
        hi, lo = split2(v)
        dot = functools.partial(jnp.dot, preferred_element_type=jnp.float32)
        y = dot(whi[...], hi) + dot(whi[...], lo) + dot(wlo[...], hi)
        y = y[:size] + swap(y[size:]) * neg
        mid[n1] = cmul(y, twc[n1], tws[n1])
        return carry

    lax.fori_loop(0, RADIX, column, 0)
    step = 32

    def block(i, carry):
        at = pl.multiple_of(i * step, step)
        rows = pl.ds(at, step)
        y = dft8([mid[n, rows, :] for n in range(RADIX)])
        for k in range(RADIX):
            v = cmul(y[k], postc[k, rows, :], posts[k, rows, :])
            if gain:
                square = v * v
                irradiance = square + swap(square)
                bleach = g[k, rows, :] / (1.0 + irradiance / FLUENCE_LIMIT)
                heat[k, rows, :] = bleach * irradiance
                v = v * jnp.exp(0.5 * GAIN_LENGTH * bleach)
            out[k, rows, :] = v
        return carry

    lax.fori_loop(0, size // step, block, 0)


def fresnel(x, tables, gain=None):
    count, width = x.shape
    size = count // RADIX
    shape = jax.ShapeDtypeStruct((RADIX, size, width), jnp.float32)
    cells = x.reshape(size, RADIX, width).transpose(1, 0, 2)
    args = (cells,) + tables
    outs = [shape]
    if gain is not None:
        args = args + (gain.reshape(RADIX, size, width),)
        outs = [shape, shape]
    result = pl.pallas_call(
        functools.partial(fresnel_body, gain is not None),
        out_shape=outs,
        in_specs=[VMEM] * len(args),
        out_specs=[VMEM] * len(outs),
        scratch_shapes=[pltpu.VMEM((RADIX, size, width), jnp.float32)],
        cost_estimate=pl.CostEstimate(
            flops=6 * 2 * size * size * RADIX * width,
            bytes_accessed=32 * count * width,
            transcendentals=0,
        ),
    )(*args)
    result = [r.reshape(count, width) for r in result]
    return result[0] if gain is None else result


def make_tables(count, w):
    size = count // RADIX

    def wave(index, modulus, scale=1.0):
        angle = (index % modulus).astype(jnp.float32) * (2.0 * math.pi / modulus)
        return scale * jnp.cos(angle), scale * jnp.sin(angle)

    def packed(pair):
        cosine, sine = pair
        cosine, sine = cosine[..., None], sine[..., None]
        shape = cosine.shape[:-1] + (w,)
        cosine = jnp.broadcast_to(cosine, shape)
        sine = jnp.broadcast_to(sine, shape)
        return (
            jnp.concatenate([cosine, cosine], axis=-1),
            jnp.concatenate([-sine, sine], axis=-1),
        )

    outer = lax.iota(jnp.int32, RADIX)[:, None]
    inner = lax.iota(jnp.int32, size)[None, :]
    n = outer + RADIX * inner
    pre = packed(wave(n * n, 2 * count))
    twiddle = packed(wave(-outer * inner, count))
    k = outer * size + inner
    post = packed(wave(k * k - count // 4, 2 * count, 1.0 / math.sqrt(count)))
    square = lax.iota(jnp.int32, size)
    matrix = jnp.concatenate(wave(-square[:, None] * square[None, :], size), axis=0)
    coarse = lax.reduce_precision(matrix, 8, 7)
    high, low = coarse.astype(jnp.bfloat16), (matrix - coarse).astype(jnp.bfloat16)
    return pre + (high, low) + twiddle + post


def sweeps_body(cells, mask, out, first):
    planes = out.shape[0]
    rows, cols = out.shape[1], out.shape[2]
    height, width = cells.shape[1], cells.shape[2]

    def around(v):
        return (
            pltpu.roll(v, 1, 0)
            + pltpu.roll(v, height - 1, 0)
            + pltpu.roll(v, 1, 1)
            + pltpu.roll(v, width - 1, 1)
        )

    first[0] = jnp.zeros((height, width), jnp.float32)
    first[planes + 1] = jnp.zeros((height, width), jnp.float32)

    def one(z, carry):
        v = cells[z + 1]
        total = v + around(v) + cells[z] + cells[z + 2]
        first[z + 1] = total * mask[...]
        return carry

    lax.fori_loop(0, planes, one, 0)

    def two(z, carry):
        total = around(first[z + 1]) + first[z] + first[z + 2]
        out[z] = (cells[z + 1, :rows, :cols] + total[:rows, :cols]) / 7.0
        return carry

    lax.fori_loop(0, planes, two, 0)


def shift(x, axis, up):
    count = lax.axis_size(axis)
    if up:
        pairs = [(i, i + 1) for i in range(count - 1)]
    else:
        pairs = [(i + 1, i) for i in range(count - 1)]
    return lax.ppermute(x, axis, pairs)


def base_temperature(start):
    tile = lax.all_to_all(start, "row", split_axis=1, concat_axis=0, tiled=True)
    planes, rows, cols = tile.shape
    top = shift(tile[:, -8:], "row", True)
    bottom = shift(tile[:, :8], "row", False)
    tall = jnp.concatenate([tile, bottom, top], axis=1)
    right = shift(jnp.swapaxes(tall[:, :, :2], 1, 2), "col", False)
    left = shift(jnp.swapaxes(tall[:, :, -2:], 1, 2), "col", True)
    gap = jnp.zeros((planes, 124, rows + 16), jnp.float32)
    side = jnp.swapaxes(jnp.concatenate([right, gap, left], axis=1), 1, 2)
    cells = jnp.pad(jnp.concatenate([tall, side], axis=2), ((1, 1), (0, 0), (0, 0)))
    height, width = cells.shape[1:]
    row_index, col_index = lax.axis_index("row"), lax.axis_index("col")
    y = lax.iota(jnp.int32, height)
    x = lax.iota(jnp.int32, width)
    y = jnp.where(y < rows + 8, y, y - height) + row_index * rows
    x = jnp.where(x < cols + 64, x, x - width) + col_index * cols
    y_ok = (y >= 0) & (y < rows * lax.axis_size("row"))
    x_ok = (x >= 0) & (x < cols * lax.axis_size("col"))
    mask = jnp.where(y_ok[:, None] & x_ok[None, :], 1.0 / 7.0, 0.0).astype(jnp.float32)
    return pl.pallas_call(
        sweeps_body,
        out_shape=jax.ShapeDtypeStruct(tile.shape, jnp.float32),
        in_specs=[VMEM, VMEM],
        out_specs=VMEM,
        scratch_shapes=[pltpu.VMEM(cells.shape, jnp.float32)],
        cost_estimate=pl.CostEstimate(
            flops=20 * cells.size, bytes_accessed=12 * cells.size, transcendentals=0
        ),
    )(cells, mask)


def around_tile(heat):
    top = shift(heat[-1:], "row", True)
    bottom = shift(heat[:1], "row", False)
    left = shift(heat[:, -1].reshape(1, -1), "col", True).reshape(-1, 1)
    right = shift(heat[:, 0].reshape(1, -1), "col", False).reshape(-1, 1)
    return (
        jnp.concatenate([top, heat[:-1]], axis=0)
        + jnp.concatenate([heat[1:], bottom], axis=0)
        + jnp.concatenate([left, heat[:, :-1]], axis=1)
        + jnp.concatenate([heat[:, 1:], right], axis=1)
    )


def shards(cosine_part, sine_part, growth, start, pick):
    nr, nc = lax.axis_size("row"), lax.axis_size("col")
    nd = nr * nc
    rows, cols = cosine_part.shape
    count = rows * nr
    w = cols // nr
    both = ("row", "col")
    tables = make_tables(count, w)
    exchange = functools.partial(lax.all_to_all, split_axis=0, concat_axis=0)

    z = jnp.concatenate(
        [cosine_part.reshape(rows, nr, w), sine_part.reshape(rows, nr, w)], axis=2
    ).transpose(1, 0, 2)
    z = exchange(z, "row").reshape(count, 2 * w)
    gain = exchange(growth.reshape(nc, w, cols), "col")
    gain = gain.transpose(0, 2, 1).reshape(count, w)
    gain = jnp.concatenate([gain, gain], axis=1)

    z = fresnel(z, tables)
    z = exchange(z.reshape(nd, w, 2 * w), both)
    z = z.reshape(nr, nc, w, 2, w).transpose(1, 0, 4, 3, 2).reshape(count, 2 * w)
    z, heat_packed = fresnel(z, tables, gain)
    z = fresnel(z, tables)
    z = z.reshape(nc, nr, w, 2 * w).transpose(1, 0, 2, 3).reshape(nd, w, 2 * w)
    z = exchange(z, both)
    z = z.reshape(nd, w, 2, w).transpose(0, 3, 2, 1).reshape(count, 2 * w)
    heat0 = heat_packed[:, :w].reshape(nc, cols, w).transpose(0, 2, 1)
    heat0 = exchange(heat0, "col").reshape(rows, cols)
    base = base_temperature(start)
    z = fresnel(z, tables)
    z = exchange(z.reshape(nr, rows, 2 * w), "row").reshape(nr, rows, 2, w)
    real_part = z[:, :, 0].transpose(1, 0, 2).reshape(rows, cols)
    imag_part = z[:, :, 1].transpose(1, 0, 2).reshape(rows, cols)

    irradiance = real_part**2 + imag_part**2
    bleach = growth / (1.0 + irradiance / FLUENCE_LIMIT)
    heat1 = bleach * irradiance
    amplify = jnp.exp(0.5 * GAIN_LENGTH * bleach)
    real_part = real_part * amplify
    imag_part = imag_part * amplify

    planes = lax.iota(jnp.int32, base.shape[0])
    warm = base
    for step, heat in enumerate((heat0, heat1)):
        here = heat / 7.0 + around_tile(heat) / 49.0
        beside = heat / 49.0
        distance = jnp.abs(planes - pick[step])
        on = (distance == 0).astype(jnp.float32)[:, None, None]
        near = (distance == 1).astype(jnp.float32)[:, None, None]
        warm = warm + on * here[None] + near * beside[None]
    angle = INDEX_SLOPE_DNDT * jnp.sum(warm, axis=0)
    warm_out = lax.all_to_all(warm, "row", split_axis=0, concat_axis=1, tiled=True)
    c, s = jnp.cos(angle), jnp.sin(angle)
    return warm_out, real_part * c - imag_part * s, real_part * s + imag_part * c


def solution(mesh):
    placed = (P("row", "col"), P("row", "col"), P("row", "col"), P("row", None, "col"), P())
    return jax.shard_map(
        shards,
        mesh=mesh,
        in_specs=placed,
        out_specs=(P("row", None, "col"), P("row", "col"), P("row", "col")),
        check_vma=False,
    )
```

```python
import functools
import math

import jax
import jax.numpy as jnp
from jax import lax
from jax.experimental import pallas as pl
from jax.experimental.pallas import tpu as pltpu
from jax.sharding import PartitionSpec as P

FLUENCE_LIMIT = 2.0
GAIN_LENGTH = 0.2
INDEX_SLOPE_DNDT = 0.3
RADIX = 8
VMEM = pl.BlockSpec(memory_space=pltpu.VMEM)


def swap(z):
    half = z.shape[-1] // 2
    if z.shape[-1] % 128 == 0:
        return pltpu.roll(z, half, z.ndim - 1)
    return jnp.concatenate([z[:, half:], z[:, :half]], axis=1)


def cmul(z, cosine, signed_sine):
    return z * cosine + swap(z) * signed_sine


def sign_row(width, first):
    lane = lax.broadcasted_iota(jnp.int32, (1, width), 1)
    return jnp.where(lane < width // 2, first, -first).astype(jnp.float32)


def dft8(z):
    width = z[0].shape[-1]
    sgn = sign_row(width, 1.0)
    root = math.sqrt(0.5)

    def rot(v):
        return swap(v) * sgn

    def dft4(p, q, r, s):
        a, b = p + r, p - r
        c, d = q + s, rot(q - s)
        return a + c, b + d, a - c, b - d

    even = dft4(z[0], z[2], z[4], z[6])
    odd = dft4(z[1], z[3], z[5], z[7])
    turned = (
        odd[0],
        (odd[1] + rot(odd[1])) * root,
        rot(odd[2]),
        (rot(odd[3]) - odd[3]) * root,
    )
    return [even[i] + turned[i] for i in range(4)] + [even[i] - turned[i] for i in range(4)]


def split2(x):
    high = x.astype(jnp.bfloat16)
    low = (x - high.astype(jnp.float32)).astype(jnp.bfloat16)
    return high, low


def dot3(high, low, x):
    hi, lo = split2(x)
    dot = functools.partial(jnp.dot, preferred_element_type=jnp.float32)
    y = dot(high[...], hi) + dot(high[...], lo) + dot(low[...], hi)
    size = y.shape[0] // 2
    return y[:size] + swap(y[size:]) * sign_row(x.shape[1], -1.0)


STEP = 16


def fresnel_body(x, prec, pres, whi, wlo, twc, tws, postc, posts, out, mid):
    size = x.shape[1]

    def column(n, carry):
        y = dot3(whi, wlo, cmul(x[n], prec[n], pres[n]))
        mid[n] = cmul(y, twc[n], tws[n])
        return carry

    lax.fori_loop(0, RADIX, column, 0)
    last_stage(size, mid, postc, posts, out)


def last_stage(size, mid, postc, posts, out):
    def block(i, carry):
        rows = pl.ds(pl.multiple_of(i * STEP, STEP), STEP)
        y = dft8([mid[n, rows, :] for n in range(RADIX)])
        for k in range(RADIX):
            out[k, rows, :] = cmul(y[k], postc[k, rows, :], posts[k, rows, :])
        return carry

    lax.fori_loop(0, size // STEP, block, 0)


def middle_body(
    x, prec, pres, whi, wlo, twc, tws, bothc, boths, postc, posts, gain, out, heat, mid
):
    size = x.shape[1]
    inverse = 1.0 / (size * RADIX)

    def first_stage(i, carry):
        rows = pl.ds(pl.multiple_of(i * STEP, STEP), STEP)
        y = dft8([cmul(x[n, rows, :], prec[n, rows, :], pres[n, rows, :]) for n in range(RADIX)])
        for k in range(RADIX):
            mid[k, rows, :] = cmul(y[k], twc[k, rows, :], tws[k, rows, :])
        return carry

    lax.fori_loop(0, size // STEP, first_stage, 0)

    def column(n, carry):
        y = dot3(whi, wlo, mid[n])
        square = y * y
        irradiance = (square + swap(square)) * inverse
        bleach = gain[n] / (1.0 + irradiance / FLUENCE_LIMIT)
        heat[n] = bleach * irradiance
        y = cmul(y * jnp.exp(0.5 * GAIN_LENGTH * bleach), bothc[n], boths[n])
        y = dot3(whi, wlo, y)
        mid[n] = cmul(y, twc[n], tws[n])
        return carry

    lax.fori_loop(0, RADIX, column, 0)
    last_stage(size, mid, postc, posts, out)


def call(body, n_out, *args):
    shape = jax.ShapeDtypeStruct(args[0].shape, jnp.float32)
    size, width = shape.shape[1:]
    return pl.pallas_call(
        body,
        out_shape=[shape] * n_out,
        in_specs=[VMEM] * len(args),
        out_specs=[VMEM] * n_out,
        scratch_shapes=[pltpu.VMEM(shape.shape, jnp.float32)],
        cost_estimate=pl.CostEstimate(
            flops=6 * 2 * size * size * RADIX * width,
            bytes_accessed=32 * shape.size,
            transcendentals=0,
        ),
    )(*args)


def fresnel(x, t):
    count, width = x.shape
    cells = x.reshape(count // RADIX, RADIX, width).transpose(1, 0, 2)
    out = call(fresnel_body, 1, cells, *t["pre"], *t["matrix"], *t["twiddle"], *t["post"])[0]
    return out.reshape(count, width)


def make_tables(count, w):
    size = count // RADIX

    def wave(index, modulus, scale=1.0):
        angle = (index % modulus).astype(jnp.float32) * (2.0 * math.pi / modulus)
        return scale * jnp.cos(angle), scale * jnp.sin(angle)

    def packed(pair):
        cosine, sine = pair
        cosine, sine = cosine[..., None], sine[..., None]
        shape = cosine.shape[:-1] + (w,)
        cosine = jnp.broadcast_to(cosine, shape)
        sine = jnp.broadcast_to(sine, shape)
        return (
            jnp.concatenate([cosine, cosine], axis=-1),
            jnp.concatenate([-sine, sine], axis=-1),
        )

    outer = lax.iota(jnp.int32, RADIX)[:, None]
    inner = lax.iota(jnp.int32, size)[None, :]
    n = outer + RADIX * inner
    k = outer * size + inner
    root = 1.0 / math.sqrt(count)
    square = lax.iota(jnp.int32, size)
    matrix = jnp.concatenate(wave(-square[:, None] * square[None, :], size), axis=0)
    coarse = lax.reduce_precision(matrix, 8, 7)
    return {
        "pre": packed(wave(n * n, 2 * count)),
        "pre_natural": packed(wave(k * k, 2 * count)),
        "both": packed(wave(2 * n * n - count // 4, 2 * count, root)),
        "twiddle": packed(wave(-outer * inner, count)),
        "post": packed(wave(k * k - count // 4, 2 * count, root)),
        "matrix": (coarse.astype(jnp.bfloat16), (matrix - coarse).astype(jnp.bfloat16)),
    }


def sweeps_body(cells, mask, out, summed, first):
    planes = out.shape[0]
    rows, cols = out.shape[1], out.shape[2]
    height, width = cells.shape[1], cells.shape[2]

    def around(v):
        return (
            pltpu.roll(v, 1, 0)
            + pltpu.roll(v, height - 1, 0)
            + pltpu.roll(v, 1, 1)
            + pltpu.roll(v, width - 1, 1)
        )

    first[0] = jnp.zeros((height, width), jnp.float32)
    first[planes + 1] = jnp.zeros((height, width), jnp.float32)

    def one(z, carry):
        v = cells[z + 1]
        total = v + around(v) + cells[z] + cells[z + 2]
        first[z + 1] = total * mask[...]
        return carry

    lax.fori_loop(0, planes, one, 0)

    def two(z, carry):
        total = around(first[z + 1]) + first[z] + first[z + 2]
        warm = (cells[z + 1, 8 : rows + 8, :cols] + total[8 : rows + 8, :cols]) / 7.0
        out[z] = warm
        summed[...] += warm
        return carry

    summed[...] = jnp.zeros_like(summed)

    lax.fori_loop(0, planes, two, 0)


def shift(x, axis, up):
    count = lax.axis_size(axis)
    if up:
        pairs = [(i, i + 1) for i in range(count - 1)]
    else:
        pairs = [(i + 1, i) for i in range(count - 1)]
    return lax.ppermute(x, axis, pairs)


def place(parts, axis):
    count, me = lax.axis_size(axis), lax.axis_index(axis)
    out = jnp.zeros((count,) + parts[0].shape, parts[0].dtype)
    for d, part in enumerate(parts):
        out = lax.dynamic_update_index_in_dim(out, part, (me - d + count) % count, 0)
    return out


def onward(x, axis, d):
    count = lax.axis_size(axis)
    return lax.ppermute(x, axis, [(i, (i + d) % count) for i in range(count)])


def gather_rows(tile):
    parts = [tile] + [onward(tile, "row", d) for d in range(1, lax.axis_size("row"))]
    return place(parts, "row").reshape(-1, tile.shape[1])


def base_temperature(start):
    nr, me = lax.axis_size("row"), lax.axis_index("row")
    local, length, cols = start.shape
    rows = length // nr
    planes = local * nr
    tall = jnp.pad(start, ((0, 0), (8, 8), (0, 0)))
    parts = []
    for d in range(nr):
        part = lax.dynamic_slice_in_dim(tall, (me + d) % nr * rows, rows + 16, 1)
        parts.append(onward(part, "row", d) if d else part)
    tall = place(parts, "row").reshape(planes, rows + 16, cols)
    right = shift(jnp.swapaxes(tall[:, :, :2], 1, 2), "col", False)
    left = shift(jnp.swapaxes(tall[:, :, -2:], 1, 2), "col", True)
    gap = jnp.zeros((planes, 124, rows + 16), jnp.float32)
    side = jnp.swapaxes(jnp.concatenate([right, gap, left], axis=1), 1, 2)
    cells = jnp.pad(jnp.concatenate([tall, side], axis=2), ((1, 1), (0, 0), (0, 0)))
    height, width = cells.shape[1:]
    row_index, col_index = lax.axis_index("row"), lax.axis_index("col")
    y = lax.iota(jnp.int32, height)
    x = lax.iota(jnp.int32, width)
    y = y - 8 + row_index * rows
    x = jnp.where(x < cols + 64, x, x - width) + col_index * cols
    y_ok = (y >= 0) & (y < rows * lax.axis_size("row"))
    x_ok = (x >= 0) & (x < cols * lax.axis_size("col"))
    mask = jnp.where(y_ok[:, None] & x_ok[None, :], 1.0 / 7.0, 0.0).astype(jnp.float32)
    base, summed = pl.pallas_call(
        sweeps_body,
        out_shape=[
            jax.ShapeDtypeStruct((planes, rows, cols), jnp.float32),
            jax.ShapeDtypeStruct((rows, cols), jnp.float32),
        ],
        in_specs=[VMEM, VMEM],
        out_specs=[VMEM, VMEM],
        scratch_shapes=[pltpu.VMEM(cells.shape, jnp.float32)],
        cost_estimate=pl.CostEstimate(
            flops=20 * cells.size, bytes_accessed=12 * cells.size, transcendentals=0
        ),
    )(cells, mask)
    slabs = base.reshape(nr, local, rows, cols)
    parts = []
    for d in range(nr):
        part = lax.dynamic_index_in_dim(slabs, (me + d) % nr, 0, keepdims=False)
        parts.append(onward(part, "row", d) if d else part)
    out = jnp.zeros(start.shape, jnp.float32)
    for d, part in enumerate(parts):
        out = lax.dynamic_update_slice_in_dim(out, part, (me - d + nr) % nr * rows, 1)
    return out, summed


def spread(heat):
    left = shift(heat[:, -1].reshape(1, -1), "col", True).reshape(-1, 1)
    right = shift(heat[:, 0].reshape(1, -1), "col", False).reshape(-1, 1)
    edge = jnp.zeros_like(heat[:1])
    around = (
        jnp.concatenate([edge, heat[:-1]], axis=0)
        + jnp.concatenate([heat[1:], edge], axis=0)
        + jnp.concatenate([left, heat[:, :-1]], axis=1)
        + jnp.concatenate([heat[:, 1:], right], axis=1)
    )
    return heat / 7.0 + around / 49.0


def shards(cosine_part, sine_part, growth, start, pick):
    nr, nc = lax.axis_size("row"), lax.axis_size("col")
    nd = nr * nc
    rows, cols = cosine_part.shape
    count = rows * nr
    w = cols // nr
    both = ("row", "col")
    tables = make_tables(count, w)
    exchange = functools.partial(lax.all_to_all, split_axis=0, concat_axis=0)

    z = jnp.concatenate(
        [cosine_part.reshape(rows, nr, w), sine_part.reshape(rows, nr, w)], axis=2
    ).transpose(1, 0, 2)
    z = exchange(z, "row").reshape(count, 2 * w)
    gain = exchange(growth.reshape(nc, w, cols), "col")
    size = count // RADIX
    gain = gain.reshape(nc, w, cols // RADIX, RADIX).transpose(3, 0, 2, 1).reshape(RADIX, size, w)
    gain = jnp.concatenate([gain, gain], axis=2)

    z = fresnel(z, tables)
    z = exchange(z.reshape(nd, w, 2 * w), both)
    z = z.reshape(nr, nc, w, 2, w).transpose(1, 0, 4, 3, 2).reshape(count, 2 * w)
    t = tables
    z, heat_packed = call(
        middle_body,
        2,
        z.reshape(RADIX, size, 2 * w),
        *t["pre_natural"],
        *t["matrix"],
        *t["twiddle"],
        *t["both"],
        *t["post"],
        gain,
    )
    z = z.reshape(nc, nr, w, 2 * w).transpose(1, 0, 2, 3).reshape(nd, w, 2 * w)
    z = exchange(z, both)
    z = z.reshape(nd, w, 2, w).transpose(0, 3, 2, 1).reshape(count, 2 * w)
    heat0 = heat_packed[:, :, :w].reshape(RADIX, nc, cols // RADIX, w).transpose(1, 3, 2, 0)
    heat0 = exchange(heat0.reshape(nc, w, cols), "col").reshape(rows, cols)
    heat0 = gather_rows(heat0)
    wide0 = spread(heat0)
    base, summed = base_temperature(start)
    z = fresnel(z, tables)
    z = exchange(z.reshape(nr, rows, 2 * w), "row").reshape(nr, rows, 2, w)
    real_part = z[:, :, 0].transpose(1, 0, 2).reshape(rows, cols)
    imag_part = z[:, :, 1].transpose(1, 0, 2).reshape(rows, cols)

    irradiance = real_part**2 + imag_part**2
    bleach = growth / (1.0 + irradiance / FLUENCE_LIMIT)
    heat1 = bleach * irradiance
    amplify = jnp.exp(0.5 * GAIN_LENGTH * bleach)
    real_part = real_part * amplify
    imag_part = imag_part * amplify

    heat1 = gather_rows(heat1)
    wide1 = spread(heat1)
    local = start.shape[0]
    me = lax.axis_index("row")
    ids = me * local + lax.iota(jnp.int32, local)
    warm = base
    for step, (heat, wide) in enumerate(((heat0, wide0), (heat1, wide1))):
        beside = heat / 49.0
        distance = jnp.abs(ids - pick[step])
        on = (distance == 0).astype(jnp.float32)[:, None, None]
        near = (distance == 1).astype(jnp.float32)[:, None, None]
        warm = warm + on * wide[None] + near * beside[None]
        inside = (pick[step] > 0).astype(jnp.float32) + (pick[step] < local * nr - 1)
        own = lax.dynamic_slice_in_dim(wide + inside * beside, me * rows, rows, 0)
        summed = summed + own
    angle = INDEX_SLOPE_DNDT * summed
    c, s = jnp.cos(angle), jnp.sin(angle)
    return warm, real_part * c - imag_part * s, real_part * s + imag_part * c


def solution(mesh):
    placed = (P("row", "col"), P("row", "col"), P("row", "col"), P("row", None, "col"), P())
    return jax.shard_map(
        shards,
        mesh=mesh,
        in_specs=placed,
        out_specs=(P("row", None, "col"), P("row", "col"), P("row", "col")),
        check_vma=False,
    )
```

```python
import functools
import math

import jax
import jax.numpy as jnp
from jax import lax
from jax.experimental import pallas as pl
from jax.experimental.pallas import tpu as pltpu
from jax.sharding import PartitionSpec as P

FLUENCE_LIMIT = 2.0
GAIN_LENGTH = 0.2
INDEX_SLOPE_DNDT = 0.3
RADIX = 8
VMEM = pl.BlockSpec(memory_space=pltpu.VMEM)


def swap(z):
    half = z.shape[-1] // 2
    if z.shape[-1] % 128 == 0:
        return pltpu.roll(z, half, z.ndim - 1)
    return jnp.concatenate([z[:, half:], z[:, :half]], axis=1)


def cmul(z, cosine, signed_sine):
    return z * cosine + swap(z) * signed_sine


def sign_row(width, first):
    lane = lax.broadcasted_iota(jnp.int32, (1, width), 1)
    return jnp.where(lane < width // 2, first, -first).astype(jnp.float32)


def dft8(z):
    width = z[0].shape[-1]
    sgn = sign_row(width, 1.0)
    root = math.sqrt(0.5)

    def rot(v):
        return swap(v) * sgn

    def dft4(p, q, r, s):
        a, b = p + r, p - r
        c, d = q + s, rot(q - s)
        return a + c, b + d, a - c, b - d

    even = dft4(z[0], z[2], z[4], z[6])
    odd = dft4(z[1], z[3], z[5], z[7])
    turned = (
        odd[0],
        (odd[1] + rot(odd[1])) * root,
        rot(odd[2]),
        (rot(odd[3]) - odd[3]) * root,
    )
    return [even[i] + turned[i] for i in range(4)] + [even[i] - turned[i] for i in range(4)]


def split2(x):
    high = x.astype(jnp.bfloat16)
    low = (x - high.astype(jnp.float32)).astype(jnp.bfloat16)
    return high, low


def dot3(matrix, columns):
    width = columns[0].shape[1]
    hi, lo = split2(jnp.concatenate(columns, axis=1))
    y = jnp.dot(
        matrix[...],
        jnp.concatenate([hi, lo, hi], axis=0),
        preferred_element_type=jnp.float32,
    )
    size = y.shape[0] // 2
    neg = sign_row(width, -1.0)
    blocks = [y[:, i * width : (i + 1) * width] for i in range(len(columns))]
    return [v[:size] + swap(v[size:]) * neg for v in blocks]


STEP = 16


def fresnel_body(x, prec, pres, wide, twc, tws, postc, posts, out, mid):
    size = x.shape[1]

    def column(i, carry):
        pair = (2 * i, 2 * i + 1)
        ys = dot3(wide, [cmul(x[n], prec[n], pres[n]) for n in pair])
        for n, y in zip(pair, ys):
            mid[n] = cmul(y, twc[n], tws[n])
        return carry

    lax.fori_loop(0, RADIX // 2, column, 0)
    last_stage(size, mid, postc, posts, out)


def last_stage(size, mid, postc, posts, out):
    def block(i, carry):
        rows = pl.ds(pl.multiple_of(i * STEP, STEP), STEP)
        y = dft8([mid[n, rows, :] for n in range(RADIX)])
        for k in range(RADIX):
            out[k, rows, :] = cmul(y[k], postc[k, rows, :], posts[k, rows, :])
        return carry

    lax.fori_loop(0, size // STEP, block, 0)


def middle_body(
    x, prec, pres, wide, twc, tws, bothc, boths, postc, posts, gain, out, heat, mid
):
    size = x.shape[1]
    inverse = 1.0 / (size * RADIX)

    def first_stage(i, carry):
        rows = pl.ds(pl.multiple_of(i * STEP, STEP), STEP)
        y = dft8([cmul(x[n, rows, :], prec[n, rows, :], pres[n, rows, :]) for n in range(RADIX)])
        for k in range(RADIX):
            mid[k, rows, :] = cmul(y[k], twc[k, rows, :], tws[k, rows, :])
        return carry

    lax.fori_loop(0, size // STEP, first_stage, 0)

    def column(i, carry):
        pair = (2 * i, 2 * i + 1)
        turned = []
        for n, y in zip(pair, dot3(wide, [mid[n] for n in pair])):
            square = y * y
            irradiance = (square + swap(square)) * inverse
            bleach = gain[n] / (1.0 + irradiance / FLUENCE_LIMIT)
            heat[n] = bleach * irradiance
            turned.append(cmul(y * jnp.exp(0.5 * GAIN_LENGTH * bleach), bothc[n], boths[n]))
        for n, y in zip(pair, dot3(wide, turned)):
            mid[n] = cmul(y, twc[n], tws[n])
        return carry

    lax.fori_loop(0, RADIX // 2, column, 0)
    last_stage(size, mid, postc, posts, out)


def call(body, n_out, *args):
    shape = jax.ShapeDtypeStruct(args[0].shape, jnp.float32)
    size, width = shape.shape[1:]
    return pl.pallas_call(
        body,
        out_shape=[shape] * n_out,
        in_specs=[VMEM] * len(args),
        out_specs=[VMEM] * n_out,
        scratch_shapes=[pltpu.VMEM(shape.shape, jnp.float32)],
        cost_estimate=pl.CostEstimate(
            flops=6 * 2 * size * size * RADIX * width,
            bytes_accessed=32 * shape.size,
            transcendentals=0,
        ),
    )(*args)


def fresnel(x, t):
    count, width = x.shape
    cells = x.reshape(count // RADIX, RADIX, width).transpose(1, 0, 2)
    out = call(fresnel_body, 1, cells, *t["pre"], *t["matrix"], *t["twiddle"], *t["post"])[0]
    return out.reshape(count, width)


def make_tables(count, w):
    size = count // RADIX

    def wave(index, modulus, scale=1.0):
        angle = (index % modulus).astype(jnp.float32) * (2.0 * math.pi / modulus)
        return scale * jnp.cos(angle), scale * jnp.sin(angle)

    def packed(pair):
        cosine, sine = pair
        cosine, sine = cosine[..., None], sine[..., None]
        shape = cosine.shape[:-1] + (w,)
        cosine = jnp.broadcast_to(cosine, shape)
        sine = jnp.broadcast_to(sine, shape)
        return (
            jnp.concatenate([cosine, cosine], axis=-1),
            jnp.concatenate([-sine, sine], axis=-1),
        )

    outer = lax.iota(jnp.int32, RADIX)[:, None]
    inner = lax.iota(jnp.int32, size)[None, :]
    n = outer + RADIX * inner
    k = outer * size + inner
    root = 1.0 / math.sqrt(count)
    square = lax.iota(jnp.int32, size)
    matrix = jnp.concatenate(wave(-square[:, None] * square[None, :], size), axis=0)
    coarse = lax.reduce_precision(matrix, 8, 7)
    high, low = coarse.astype(jnp.bfloat16), (matrix - coarse).astype(jnp.bfloat16)
    return {
        "pre": packed(wave(n * n, 2 * count)),
        "pre_natural": packed(wave(k * k, 2 * count)),
        "both": packed(wave(2 * n * n - count // 4, 2 * count, root)),
        "twiddle": packed(wave(-outer * inner, count)),
        "post": packed(wave(k * k - count // 4, 2 * count, root)),
        "matrix": (jnp.concatenate([high, high, low], axis=1),),
    }


def sweeps_body(cells, mask, out, summed, first):
    planes = out.shape[0]
    rows, cols = out.shape[1], out.shape[2]
    height, width = cells.shape[1], cells.shape[2]

    def around(v):
        return (
            pltpu.roll(v, 1, 0)
            + pltpu.roll(v, height - 1, 0)
            + pltpu.roll(v, 1, 1)
            + pltpu.roll(v, width - 1, 1)
        )

    first[0] = jnp.zeros((height, width), jnp.float32)
    first[planes + 1] = jnp.zeros((height, width), jnp.float32)

    def one(z, carry):
        v = cells[z + 1]
        total = v + around(v) + cells[z] + cells[z + 2]
        first[z + 1] = total * mask[...]
        return carry

    lax.fori_loop(0, planes, one, 0)

    def two(z, carry):
        total = around(first[z + 1]) + first[z] + first[z + 2]
        warm = (cells[z + 1, 8 : rows + 8, :cols] + total[8 : rows + 8, :cols]) / 7.0
        out[z] = warm
        summed[...] += warm
        return carry

    summed[...] = jnp.zeros_like(summed)

    lax.fori_loop(0, planes, two, 0)


def shift(x, axis, up):
    count = lax.axis_size(axis)
    if up:
        pairs = [(i, i + 1) for i in range(count - 1)]
    else:
        pairs = [(i + 1, i) for i in range(count - 1)]
    return lax.ppermute(x, axis, pairs)


def place(parts, axis):
    count, me = lax.axis_size(axis), lax.axis_index(axis)
    out = jnp.zeros((count,) + parts[0].shape, parts[0].dtype)
    for d, part in enumerate(parts):
        out = lax.dynamic_update_index_in_dim(out, part, (me - d + count) % count, 0)
    return out


def onward(x, axis, d):
    count = lax.axis_size(axis)
    return lax.ppermute(x, axis, [(i, (i + d) % count) for i in range(count)])


def gather_rows(tile):
    parts = [tile] + [onward(tile, "row", d) for d in range(1, lax.axis_size("row"))]
    return place(parts, "row").reshape(-1, tile.shape[1])


def base_temperature(start):
    nr, me = lax.axis_size("row"), lax.axis_index("row")
    local, length, cols = start.shape
    rows = length // nr
    planes = local * nr
    tall = jnp.pad(start, ((0, 0), (8, 8), (0, 0)))
    parts = []
    for d in range(nr):
        part = lax.dynamic_slice_in_dim(tall, (me + d) % nr * rows, rows + 16, 1)
        parts.append(onward(part, "row", d) if d else part)
    tall = place(parts, "row").reshape(planes, rows + 16, cols)
    right = shift(jnp.swapaxes(tall[:, :, :2], 1, 2), "col", False)
    left = shift(jnp.swapaxes(tall[:, :, -2:], 1, 2), "col", True)
    gap = jnp.zeros((planes, 124, rows + 16), jnp.float32)
    side = jnp.swapaxes(jnp.concatenate([right, gap, left], axis=1), 1, 2)
    cells = jnp.pad(jnp.concatenate([tall, side], axis=2), ((1, 1), (0, 0), (0, 0)))
    height, width = cells.shape[1:]
    row_index, col_index = lax.axis_index("row"), lax.axis_index("col")
    y = lax.iota(jnp.int32, height)
    x = lax.iota(jnp.int32, width)
    y = y - 8 + row_index * rows
    x = jnp.where(x < cols + 64, x, x - width) + col_index * cols
    y_ok = (y >= 0) & (y < rows * lax.axis_size("row"))
    x_ok = (x >= 0) & (x < cols * lax.axis_size("col"))
    mask = jnp.where(y_ok[:, None] & x_ok[None, :], 1.0 / 7.0, 0.0).astype(jnp.float32)
    base, summed = pl.pallas_call(
        sweeps_body,
        name="sweeps",
        out_shape=[
            jax.ShapeDtypeStruct((planes, rows, cols), jnp.float32),
            jax.ShapeDtypeStruct((rows, cols), jnp.float32),
        ],
        in_specs=[VMEM, VMEM],
        out_specs=[VMEM, VMEM],
        scratch_shapes=[pltpu.VMEM(cells.shape, jnp.float32)],
        cost_estimate=pl.CostEstimate(
            flops=20 * cells.size, bytes_accessed=12 * cells.size, transcendentals=0
        ),
    )(cells, mask)
    slabs = base.reshape(nr, local, rows, cols)
    parts = []
    for d in range(nr):
        part = lax.dynamic_index_in_dim(slabs, (me + d) % nr, 0, keepdims=False)
        parts.append(onward(part, "row", d) if d else part)
    out = jnp.zeros(start.shape, jnp.float32)
    for d, part in enumerate(parts):
        out = lax.dynamic_update_slice_in_dim(out, part, (me - d + nr) % nr * rows, 1)
    return out, summed


def spread(heat):
    left = shift(heat[:, -1].reshape(1, -1), "col", True).reshape(-1, 1)
    right = shift(heat[:, 0].reshape(1, -1), "col", False).reshape(-1, 1)
    edge = jnp.zeros_like(heat[:1])
    around = (
        jnp.concatenate([edge, heat[:-1]], axis=0)
        + jnp.concatenate([heat[1:], edge], axis=0)
        + jnp.concatenate([left, heat[:, :-1]], axis=1)
        + jnp.concatenate([heat[:, 1:], right], axis=1)
    )
    return heat / 7.0 + around / 49.0


def shards(cosine_part, sine_part, growth, start, pick):
    nr, nc = lax.axis_size("row"), lax.axis_size("col")
    nd = nr * nc
    rows, cols = cosine_part.shape
    count = rows * nr
    w = cols // nr
    both = ("row", "col")
    tables = make_tables(count, w)
    exchange = functools.partial(lax.all_to_all, split_axis=0, concat_axis=0)

    z = jnp.concatenate(
        [cosine_part.reshape(rows, nr, w), sine_part.reshape(rows, nr, w)], axis=2
    ).transpose(1, 0, 2)
    z = exchange(z, "row").reshape(count, 2 * w)
    gain = exchange(growth.reshape(nc, w, cols), "col")
    size = count // RADIX
    gain = gain.reshape(nc, w, cols // RADIX, RADIX).transpose(3, 0, 2, 1).reshape(RADIX, size, w)
    gain = jnp.concatenate([gain, gain], axis=2)

    z = fresnel(z, tables)
    z = exchange(z.reshape(nd, w, 2 * w), both)
    z = z.reshape(nr, nc, w, 2, w).transpose(1, 0, 4, 3, 2).reshape(count, 2 * w)
    t = tables
    z, heat_packed = call(
        middle_body,
        2,
        z.reshape(RADIX, size, 2 * w),
        *t["pre_natural"],
        *t["matrix"],
        *t["twiddle"],
        *t["both"],
        *t["post"],
        gain,
    )
    z = z.reshape(nc, nr, w, 2 * w).transpose(1, 0, 2, 3).reshape(nd, w, 2 * w)
    z = exchange(z, both)
    z = z.reshape(nd, w, 2, w).transpose(0, 3, 2, 1).reshape(count, 2 * w)
    heat0 = heat_packed[:, :, :w].reshape(RADIX, nc, cols // RADIX, w).transpose(1, 3, 2, 0)
    heat0 = exchange(heat0.reshape(nc, w, cols), "col").reshape(rows, cols)
    heat0 = gather_rows(heat0)
    wide0 = spread(heat0)
    base, summed = base_temperature(start)
    z = fresnel(z, tables)
    z = exchange(z.reshape(nr, rows, 2 * w), "row").reshape(nr, rows, 2, w)
    real_part = z[:, :, 0].transpose(1, 0, 2).reshape(rows, cols)
    imag_part = z[:, :, 1].transpose(1, 0, 2).reshape(rows, cols)

    irradiance = real_part**2 + imag_part**2
    bleach = growth / (1.0 + irradiance / FLUENCE_LIMIT)
    heat1 = bleach * irradiance
    amplify = jnp.exp(0.5 * GAIN_LENGTH * bleach)
    real_part = real_part * amplify
    imag_part = imag_part * amplify

    heat1 = gather_rows(heat1)
    wide1 = spread(heat1)
    local = start.shape[0]
    me = lax.axis_index("row")
    ids = me * local + lax.iota(jnp.int32, local)
    warm = base
    for step, (heat, wide) in enumerate(((heat0, wide0), (heat1, wide1))):
        beside = heat / 49.0
        distance = jnp.abs(ids - pick[step])
        on = (distance == 0).astype(jnp.float32)[:, None, None]
        near = (distance == 1).astype(jnp.float32)[:, None, None]
        warm = warm + on * wide[None] + near * beside[None]
        inside = (pick[step] > 0).astype(jnp.float32) + (pick[step] < local * nr - 1)
        own = lax.dynamic_slice_in_dim(wide + inside * beside, me * rows, rows, 0)
        summed = summed + own
    angle = INDEX_SLOPE_DNDT * summed
    c, s = jnp.cos(angle), jnp.sin(angle)
    return warm, real_part * c - imag_part * s, real_part * s + imag_part * c


def solution(mesh):
    placed = (P("row", "col"), P("row", "col"), P("row", "col"), P("row", None, "col"), P())
    return jax.shard_map(
        shards,
        mesh=mesh,
        in_specs=placed,
        out_specs=(P("row", None, "col"), P("row", "col"), P("row", "col")),
        check_vma=False,
    )
```
